32 devices in a mesh: groups: 2 (over y), dp: 2 (over core), tensor: 8 (over z, x).
Axes of the slice: x: 2, y: 2, z: 4, core: 2. Of those that a mesh axis runs over, the one named last changes fastest.
Arguments:
- tokens: bfloat16 [512, 8192], P(('groups', 'dp', 'tensor')), parts along dimension 0, may hold values from -134 to 134
- ln_gain: float32 [8192], replicated, may hold values from 0.25 to 1.75
- gate_weight: bfloat16 [8192, 16384], P('dp', 'tensor'), may hold values from -0.09375 to 0.09375
- up_weight: bfloat16 [8192, 16384], P('dp', 'tensor'), may hold values from -0.09375 to 0.09375
- down_weight: bfloat16 [16384, 8192], P('tensor', 'dp'), may hold values from -0.0625 to 0.0625
- gate_mask: int32 [64, 128], replicated, may hold values from 0 to 1, as said below
- up_mask: int32 [64, 128], replicated, may hold values from 0 to 1, as said below
- down_mask: int32 [128, 64], replicated, may hold values from 0 to 1, as said below
Outputs:
- mlp_out: bfloat16 [512, 8192], P(('groups', 'dp', 'tensor')), parts along dimension 0
The draws below stay inside these ranges and needn't reach their ends.
There are 2 independent parts, one for each index of `groups`. The reference program is written for one: setup_inputs(seed, part) draws one part's arguments, and reference() takes and returns one part's arrays. A program takes and returns all parts, laid end to end along the dimension named above; an argument that names none is the same for every part. Nothing has to cross between parts.
Inputs may be any that keep to these rules, and one draw needn't show every extreme that they name: `gate_mask`: in every block column, each of the 2 owners' runs of 32 consecutive block rows holds at least one and at most 24 ones; in some column every owner's run holds exactly 24. `up_mask`: as gate_mask. `down_mask`: in every block row, each of the 2 owners' runs of 32 consecutive block columns holds at least one and at most 24 ones; in some row every owner's run holds exactly 24.
All inputs are finite; a program needn't handle non-finite values.
Results may differ from the reference program's by a relative error of at most 0.0065.
Values may be sent and summed in bfloat16 or wider, within the bound.
A program may use at most 448 MiB of HBM per device.

```python
import math
import jax
import jax.numpy as jnp
from jax import lax

D = 8192
FF = 16384
BLK = 128
CAP = 24
TOKENS = 256
DB = 64
FB = 128
OWN_BLOCKS = 32


def draw_tokens(key, part):
    subkeys = jax.random.split(key, 3)
    row_scale = jnp.exp(jax.random.uniform(subkeys[0], (TOKENS, 1), jnp.float32, 0.0, math.log(10.0)))
    column_scale = jnp.exp(jax.random.uniform(subkeys[1], (1, D), jnp.float32, 0.0, math.log(10.0)))
    pattern = jnp.clip(jax.random.normal(subkeys[2], (TOKENS, D), jnp.float32), -4.0, 4.0)
    return (pattern * row_scale * column_scale / 3.0).astype(jnp.bfloat16)


def tile_mask(key, matrix_id):
    subkey = jax.random.fold_in(key, matrix_id)
    key_counts, key_fullest, key_scores = jax.random.split(subkey, 3)
    owners = DB // OWN_BLOCKS
    lowest = max(1, OWN_BLOCKS // 8)
    counts = jax.random.randint(key_counts, (owners, FB), lowest, CAP + 1)
    fullest = jax.random.randint(key_fullest, (), 0, FB)
    counts = jnp.where(jnp.arange(FB)[None, :] == fullest, CAP, counts)
    scores = jax.random.randint(key_scores, (owners, FB, OWN_BLOCKS), 0, 1 << 20) * OWN_BLOCKS
    scores = scores + jnp.arange(OWN_BLOCKS)[None, None, :]
    ranking = jnp.argsort(jnp.argsort(scores, axis=-1), axis=-1)
    return (ranking < counts[:, :, None]).astype(jnp.int32)


def draw_gate_mask(key, part):
    return tile_mask(key, 1).transpose(0, 2, 1).reshape(DB, FB)


def draw_up_mask(key, part):
    return tile_mask(key, 2).transpose(0, 2, 1).reshape(DB, FB)


def draw_down_mask(key, part):
    return tile_mask(key, 3).transpose(1, 0, 2).reshape(FB, DB)


def steps_of(key, shape, cuts, smallest, top_value):
    loudness = 1.0
    for position, shards_of in cuts:
        steps = jax.random.uniform(jax.random.fold_in(jax.random.fold_in(key, 6), position), (shards_of,), jnp.float32, smallest / len(cuts), top_value / len(cuts))
        loudness = loudness * jnp.repeat(jnp.exp(steps), shape[position] // shards_of).reshape((-1,) + (1,) * (len(shape) - 1 - position))
    return loudness


def normal_values(key, extent, spread, reach, pieces=(), held_as=jnp.bfloat16):
    array = spread * jax.random.normal(key, extent, jnp.float32)
    if pieces:
        array = array * steps_of(key, extent, pieces, -0.22, 0.18)
    return jnp.clip(array, -reach, reach).astype(held_as)


def setup_inputs(seed: int = 0, part: int = 0) -> dict:
    seeds = jax.random.split(jax.random.key(seed), 9)
    part_keys = jax.random.split(jax.random.fold_in(seeds[8], part), 9)
    return {
        "tokens": draw_tokens(jax.random.fold_in(jax.random.fold_in(seeds[8], part), 71), part),
        "ln_gain": jnp.clip(1.0 + 0.15 * jax.random.normal(seeds[1], (D,), jnp.float32), 0.25, 1.75),
        "gate_weight": normal_values(seeds[2], (D, FF), (D // 2) ** -0.5, 0.09375, ((0, 2), (1, 8))),
        "up_weight": normal_values(seeds[3], (D, FF), (D // 2) ** -0.5, 0.09375, ((0, 2), (1, 8))),
        "down_weight": normal_values(seeds[4], (FF, D), (FF // 2) ** -0.5, 0.0625, ((0, 8), (1, 2))),
        "gate_mask": draw_gate_mask(jax.random.fold_in(seeds[8], 71), part),
        "up_mask": draw_up_mask(jax.random.fold_in(seeds[8], 71), part),
        "down_mask": draw_down_mask(jax.random.fold_in(seeds[8], 71), part),
    }


def masked_weight(weight, block_mask):
    row_blocks, column_blocks = block_mask.shape
    tiled_weight = weight.reshape(row_blocks, BLK, column_blocks, BLK) * block_mask[:, None, :, None].astype(weight.dtype)
    return tiled_weight.reshape(row_blocks * BLK, column_blocks * BLK)

def reference(tokens, ln_gain, gate_weight, up_weight, down_weight, gate_mask, up_mask, down_mask):
    values = tokens.astype(jnp.float32)
    average = lax.optimization_barrier(jnp.mean(values, axis=1, keepdims=True))
    centered = values - average
    variance = lax.optimization_barrier(jnp.mean(centered * centered, axis=1, keepdims=True))
    normed = (centered * jax.lax.rsqrt(variance + 1e-05) * ln_gain).astype(jnp.bfloat16)
    gate_sums = jnp.dot(normed, masked_weight(gate_weight, gate_mask), preferred_element_type=jnp.float32)
    up_sums = jnp.dot(normed, masked_weight(up_weight, up_mask), preferred_element_type=jnp.float32)
    hidden = (jax.nn.silu(gate_sums) * up_sums).astype(jnp.bfloat16)
    mlp_out = jnp.dot(hidden, masked_weight(down_weight, down_mask), preferred_element_type=jnp.float32)
    return mlp_out.astype(jnp.bfloat16)
```

```python
import functools

import jax
import jax.numpy as jnp
from jax import lax
from jax.experimental import pallas as pl
from jax.experimental.pallas import tpu as pltpu
from jax.sharding import PartitionSpec as P

BLK = 128
ROWS = 16
NC = 256
GRP = 512
DCH = 1024
EPSILON = 1e-05
F32 = jnp.float32
BF16 = jnp.bfloat16


def layer_norm(tokens, ln_gain):
    values = tokens.astype(F32)
    average = jnp.mean(values, axis=1, keepdims=True)
    centered = values - average
    variance = jnp.mean(centered * centered, axis=1, keepdims=True)
    return (centered * lax.rsqrt(variance + EPSILON) * ln_gain).astype(BF16)


def expand(mask, dtype):
    return jnp.repeat(jnp.repeat(mask.astype(dtype), BLK, axis=0), BLK, axis=1)


def general(tokens, ln_gain, gate_weight, up_weight, down_weight, gate_mask, up_mask, down_mask):
    t = lax.axis_index("tensor")
    d = lax.axis_index("dp")
    kl, fl = gate_weight.shape
    kb, fb = kl // BLK, fl // BLK
    normed = layer_norm(tokens, ln_gain)
    rows = lax.all_gather(normed, ("dp", "tensor"), axis=0, tiled=True)
    mine = lax.dynamic_slice_in_dim(rows, d * kl, kl, 1)

    def cut(mask, r0, c0, nr, nc):
        return expand(lax.dynamic_slice(mask, (r0, c0), (nr, nc)), BF16)

    gw = gate_weight * cut(gate_mask, d * kb, t * fb, kb, fb)
    uw = up_weight * cut(up_mask, d * kb, t * fb, kb, fb)
    dw = down_weight * cut(down_mask, t * fb, d * kb, fb, kb)
    gate = lax.psum(jnp.dot(mine, gw, preferred_element_type=F32), "dp")
    up = lax.psum(jnp.dot(mine, uw, preferred_element_type=F32), "dp")
    hidden = (jax.nn.silu(gate) * up).astype(BF16)
    part = jnp.dot(hidden, dw, preferred_element_type=F32)
    full = lax.all_gather(part, "dp", axis=1, tiled=True)
    half = full.shape[0] // lax.axis_size("dp")
    full = lax.dynamic_slice_in_dim(full, d * half, half, 0)
    return lax.psum_scatter(full, "tensor", scatter_dimension=0, tiled=True).astype(BF16)


def fused_kernel(
    Z,
    gm, um, dm, tok, gain, gw_hbm, uw_hbm, dw_hbm,
    out,
    gw, uw, dw, nrm, xbuf, exs, exr, own, hid, sb, acc, rx, zs, zr, fin, finrx,
    w_sem, in_s, in_r, agz_s, agz_r, agx_s, agx_r, ex_s, ex_r, hd_s, hd_r,
    rx_s, rx_r, rz_s, rz_r, fn_s, fn_r,
):
    kl, fl = gw.shape
    kb, fb = kl // BLK, fl // BLK
    half = fl // 2
    line = Z * ROWS
    groups = half // GRP
    chunks = kl // DCH
    d = lax.axis_index("dp")
    t = lax.axis_index("tensor")
    z = t // 2
    x = t % 2
    peer = {"dp": 1 - d}
    xnbr = {"tensor": z * 2 + (1 - x)}

    def zdev(i):
        return {"tensor": lax.rem(z + i, Z) * 2 + x}

    def zsrc(i):
        return lax.rem(z + Z - i, Z)

    def slot(j):
        return pl.ds(pl.multiple_of(j * ROWS, ROWS), ROWS)

    def remote(src, dst, ss, rs, dev):
        return pltpu.make_async_remote_copy(
            src_ref=src, dst_ref=dst, send_sem=ss, recv_sem=rs,
            device_id=dev, device_id_type=pl.DeviceIdType.MESH,
        )

    def wcopy(k):
        which, part = k // 4, k % 4
        src, dst = ((gw_hbm, gw), (uw_hbm, uw), (dw_hbm, dw))[which]
        n = src.shape[0] // 4
        return pltpu.make_async_copy(
            src.at[pl.ds(part * n, n), :], dst.at[pl.ds(part * n, n), :], w_sem.at[k]
        )

    for k in range(12):
        wcopy(k).start()

    barrier = pltpu.get_barrier_semaphore()
    for dev in [peer, xnbr] + [zdev(i) for i in range(1, Z)]:
        pl.semaphore_signal(barrier, inc=1, device_id=dev, device_id_type=pl.DeviceIdType.MESH)

    values = tok[...].astype(F32)
    average = jnp.mean(values, axis=1, keepdims=True)
    centered = values - average
    variance = jnp.mean(centered * centered, axis=1, keepdims=True)
    nrm[...] = (centered * lax.rsqrt(variance + EPSILON) * gain[...]).astype(BF16)

    pl.semaphore_wait(barrier, Z + 1)

    def cols(o):
        return pl.ds(pl.multiple_of(o * kl, kl), kl)

    first = remote(nrm.at[:, cols(1 - d)], xbuf.at[d, slot(z), :], in_s, in_r, peer)
    first.start()
    xbuf[d, slot(z), :] = nrm[:, cols(d)]
    remote(nrm.at[:, cols(d)], xbuf.at[1 - d, slot(z), :], in_s, in_r, peer).wait_recv()

    def agz(h, i):
        return remote(xbuf.at[h, slot(z), :], xbuf.at[h, slot(z), :],
                      agz_s.at[h, i - 1], agz_r.at[h, i - 1], zdev(i))

    def agz_in(h, i):
        blk = xbuf.at[h, slot(zsrc(i)), :]
        return remote(blk, blk, agz_s.at[h, i - 1], agz_r.at[h, i - 1], zdev(i))

    def agx(h, i):
        return remote(xbuf.at[h, slot(zsrc(i)), :], xbuf.at[h, slot(Z + zsrc(i)), :],
                      agx_s.at[h, i], agx_r.at[h, i], xnbr)

    def ag_start(h):
        agx(h, 0).start()
        for i in range(1, Z):
            agz(h, i).start()

    def ag_forward(h, i):
        agz_in(h, i).wait_recv()
        agx(h, i).start()

    def ag_finish(h):
        for i in range(Z):
            agx(h, i).wait_recv()

    def prune(k):
        wcopy(k).wait()
        which, part = k // 4, k % 4
        w = (gw, uw, dw)[which]
        m = (gm, um, dm)[which]
        nr, nc = w.shape[0] // BLK, w.shape[1] // BLK
        if which == 2:
            r0, c0 = t * nr, d * nc
        else:
            r0, c0 = d * nr, t * nc
        n = nr // 4

        def body(b, carry):
            rb = part * n + b
            rows = pl.ds(pl.multiple_of(rb * BLK, BLK), BLK)
            for cb in range(nc):
                keep = jnp.full((16, BLK), m[r0 + rb, c0 + cb].astype(F32), F32).astype(BF16)
                tile = w[rows, cb * BLK:(cb + 1) * BLK].reshape(BLK // 16, 16, BLK)
                w[rows, cb * BLK:(cb + 1) * BLK] = (tile * keep[None]).reshape(BLK, BLK)
            return carry

        lax.fori_loop(0, n, body, 0)

    def group(h, q, mine):
        base = (d if mine else 1 - d) * half + q * GRP

        def body(c, carry):
            cs = pl.ds(pl.multiple_of(base + c * NC, NC), NC)
            g = jnp.dot(xbuf[h], gw[:, cs], preferred_element_type=F32)
            u = jnp.dot(xbuf[h], uw[:, cs], preferred_element_type=F32)
            os = pl.ds(pl.multiple_of(c * NC, NC), NC)
            dst = own if mine else exs
            dst[q, 0, :, os] = g
            dst[q, 1, :, os] = u
            return carry

        lax.fori_loop(0, GRP // NC, body, 0)
        if not mine:
            ex(h, q).start()

    def ex(h, q):
        return remote(exs.at[q], exr.at[q], ex_s.at[h, q], ex_r.at[h, q], peer)

    def hcols(o, q):
        return pl.ds(pl.multiple_of(o * half + q * GRP, GRP), GRP)

    def hd(h, q, o):
        blk = hid.at[:, hcols(o, q)]
        return remote(blk, blk, hd_s.at[h, q], hd_r.at[h, q], peer)

    def hidden(h):
        for q in range(groups):
            ex(h, q).wait()
            g = own[q, 0] + exr[q, 0]
            u = own[q, 1] + exr[q, 1]
            hid[:, hcols(d, q)] = (g / (1.0 + jnp.exp(-g)) * u).astype(BF16)
            hd(h, q, d).start()
        for q in range(groups):
            hd(h, q, 1 - d).wait_recv()

    def chunk(c):
        return pl.ds(c * DCH, DCH)

    def rsx(h, c):
        return remote(sb.at[:, chunk(c)], rx.at[h, :, chunk(c)], rx_s.at[h, c], rx_r.at[h, c], xnbr)

    def down(h):
        for c in range(chunks):
            def body(j, carry):
                cs = pl.ds(pl.multiple_of(c * DCH + j * NC, NC), NC)
                p = jnp.dot(hid[...], dw[:, cs], preferred_element_type=F32)
                acc[:, cs] = p[:line]
                sb[:, cs] = p[line:].astype(BF16)
                return carry

            lax.fori_loop(0, DCH // NC, body, 0)
            rsx(h, c).start()
        for q in range(groups):
            hd(h, q, d).wait_send()

    def rsz(h, c, i):
        return remote(zs.at[slot(lax.rem(z + i, Z)), chunk(c)], zr.at[h, i - 1, :, chunk(c)],
                      rz_s.at[h, c, i - 1], rz_r.at[h, c, i - 1], zdev(i))

    def rs_step(h, c):
        rsx(h, c).wait()
        total = acc[:, chunk(c)] + rx[h, :, chunk(c)].astype(F32)
        acc[:, chunk(c)] = total
        zs[:, chunk(c)] = total.astype(BF16)
        for i in range(1, Z):
            rsz(h, c, i).start()

    def rs_final(h):
        for c in range(chunks):
            for i in range(1, Z):
                rsz(h, c, i).wait()
            total = acc[slot(z), chunk(c)]
            for i in range(1, Z):
                total = total + zr[h, i - 1, :, chunk(c)].astype(F32)
            fin[h, :, chunk(c)] = total.astype(BF16)

    ag_start(0)
    order = list(range(12))
    per = 2
    for i in range(1, Z):
        for k in order[:per]:
            prune(k)
        order = order[per:]
        ag_forward(0, i)
    ag_start(1)
    for k in order:
        prune(k)
    ag_finish(0)
    plan = [(q, False) for q in range(groups)] + [(q, True) for q in range(groups)]
    for n, (q, mine) in enumerate(plan):
        group(0, q, mine)
        if n + 1 < Z:
            ag_forward(1, n + 1)
    hidden(0)
    down(0)
    ag_finish(1)
    for n, (q, mine) in enumerate(plan):
        group(1, q, mine)
        rs_step(0, n)
    hidden(1)
    rs_final(0)
    down(1)
    for c in range(chunks):
        rs_step(1, c)
    rs_final(1)

    last = remote(fin.at[1 - d], finrx, fn_s, fn_r, peer)
    last.start()
    out[:, cols(d)] = fin[d]
    last.wait()
    out[:, cols(1 - d)] = finrx[...]
    first.wait_send()
    for h in range(2):
        for i in range(Z):
            agx(h, i).wait_send()
        for i in range(1, Z):
            agz(h, i).wait_send()


def fused(Z, tokens, ln_gain, gate_weight, up_weight, down_weight, gate_mask, up_mask, down_mask):
    kl, fl = gate_weight.shape
    dim = tokens.shape[1]
    half = fl // 2
    groups = half // GRP
    chunks = kl // DCH
    line = Z * ROWS
    m = 2 * line
    dma = pltpu.SemaphoreType.DMA
    vm = pl.BlockSpec(memory_space=pltpu.VMEM)
    sm = pl.BlockSpec(memory_space=pltpu.SMEM)
    hbm = pl.BlockSpec(memory_space=pl.ANY)
    flops = 2 * 2 * m * kl * fl * 3
    return pl.pallas_call(
        functools.partial(fused_kernel, Z),
        out_shape=jax.ShapeDtypeStruct((ROWS, dim), BF16),
        in_specs=[sm, sm, sm, vm, vm, hbm, hbm, hbm],
        out_specs=vm,
        scratch_shapes=[
            pltpu.VMEM((kl, fl), BF16),
            pltpu.VMEM((kl, fl), BF16),
            pltpu.VMEM((fl, kl), BF16),
            pltpu.VMEM((ROWS, dim), BF16),
            pltpu.VMEM((2, m, kl), BF16),
            pltpu.VMEM((groups, 2, m, GRP), F32),
            pltpu.VMEM((groups, 2, m, GRP), F32),
            pltpu.VMEM((groups, 2, m, GRP), F32),
            pltpu.VMEM((m, fl), BF16),
            pltpu.VMEM((line, kl), BF16),
            pltpu.VMEM((line, kl), F32),
            pltpu.VMEM((2, line, kl), BF16),
            pltpu.VMEM((line, kl), BF16),
            pltpu.VMEM((2, Z - 1, ROWS, kl), BF16),
            pltpu.VMEM((2, ROWS, kl), BF16),
            pltpu.VMEM((ROWS, kl), BF16),
            dma((12,)),
            dma, dma,
            dma((2, Z - 1)), dma((2, Z - 1)),
            dma((2, Z)), dma((2, Z)),
            dma((2, groups)), dma((2, groups)),
            dma((2, groups)), dma((2, groups)),
            dma((2, chunks)), dma((2, chunks)),
            dma((2, chunks, Z - 1)), dma((2, chunks, Z - 1)),
            dma, dma,
        ],
        compiler_params=pltpu.CompilerParams(
            collective_id=0, has_side_effects=True, vmem_limit_bytes=63 * 1024 * 1024
        ),
        cost_estimate=pl.CostEstimate(
            flops=flops, bytes_accessed=6 * kl * fl, transcendentals=0
        ),
    )(gate_mask, up_mask, down_mask, tokens, ln_gain.reshape(1, dim),
      gate_weight, up_weight, down_weight)


def solution(mesh):
    tensor = mesh.shape["tensor"]
    owners = mesh.shape["dp"]
    copies = mesh.shape["groups"]
    Z = tensor // 2

    def per_device(tokens, ln_gain, gate_weight, *rest):
        rows = tokens.shape[0]
        kl, fl = gate_weight.shape
        fits = (
            owners == 2 and tensor == 2 * Z and rows == ROWS and Z == 4
            and kl == 4 * DCH and fl == 4 * GRP
        )
        if fits:
            return fused(Z, tokens, ln_gain, gate_weight, *rest)
        return general(tokens, ln_gain, gate_weight, *rest)

    in_specs = (
        P(("groups", "dp", "tensor"), None),
        P(),
        P("dp", "tensor"),
        P("dp", "tensor"),
        P("tensor", "dp"),
        P(),
        P(),
        P(),
    )
    out_specs = P(("groups", "dp", "tensor"), None)
    return jax.shard_map(
        per_device, mesh=mesh, in_specs=in_specs, out_specs=out_specs, check_vma=False
    )
```

```python
import functools

import jax
import jax.numpy as jnp
from jax import lax
from jax.experimental import pallas as pl
from jax.experimental.pallas import tpu as pltpu
from jax.sharding import PartitionSpec as P

BLK = 128
ROWS = 16
NC = 256
GRP = 512
DCH = 1024
AHEAD = 4
SUB = 2
EPSILON = 1e-05
F32 = jnp.float32
BF16 = jnp.bfloat16


def layer_norm(tokens, ln_gain):
    values = tokens.astype(F32)
    average = jnp.mean(values, axis=1, keepdims=True)
    centered = values - average
    variance = jnp.mean(centered * centered, axis=1, keepdims=True)
    return (centered * lax.rsqrt(variance + EPSILON) * ln_gain).astype(BF16)


def expand(mask, dtype):
    return jnp.repeat(jnp.repeat(mask.astype(dtype), BLK, axis=0), BLK, axis=1)


def general(tokens, ln_gain, gate_weight, up_weight, down_weight, gate_mask, up_mask, down_mask):
    t = lax.axis_index("tensor")
    d = lax.axis_index("dp")
    kl, fl = gate_weight.shape
    kb, fb = kl // BLK, fl // BLK
    normed = layer_norm(tokens, ln_gain)
    rows = lax.all_gather(normed, ("dp", "tensor"), axis=0, tiled=True)
    mine = lax.dynamic_slice_in_dim(rows, d * kl, kl, 1)

    def cut(mask, r0, c0, nr, nc):
        return expand(lax.dynamic_slice(mask, (r0, c0), (nr, nc)), BF16)

    gw = gate_weight * cut(gate_mask, d * kb, t * fb, kb, fb)
    uw = up_weight * cut(up_mask, d * kb, t * fb, kb, fb)
    dw = down_weight * cut(down_mask, t * fb, d * kb, fb, kb)
    gate = lax.psum(jnp.dot(mine, gw, preferred_element_type=F32), "dp")
    up = lax.psum(jnp.dot(mine, uw, preferred_element_type=F32), "dp")
    hidden = (jax.nn.silu(gate) * up).astype(BF16)
    part = jnp.dot(hidden, dw, preferred_element_type=F32)
    full = lax.all_gather(part, "dp", axis=1, tiled=True)
    half = full.shape[0] // lax.axis_size("dp")
    full = lax.dynamic_slice_in_dim(full, d * half, half, 0)
    return lax.psum_scatter(full, "tensor", scatter_dimension=0, tiled=True).astype(BF16)


def fused_kernel(
    Z,
    gm, um, dm, tok, gain, gw_hbm, uw_hbm, dw_hbm,
    out,
    gw, uw, dw, nrm, xbuf, exs, exr, own, hid, sb, acc, rx, zs, zr, fin, finrx,
    w_sem, in_s, in_r, agz_s, agz_r, agx_s, agx_r, ex_s, ex_r, hd_s, hd_r,
    rx_s, rx_r, rz_s, rz_r, fn_s, fn_r,
):
    kl, fl = gw.shape
    kb, fb = kl // BLK, fl // BLK
    half = fl // 2
    line = Z * ROWS
    groups = half // GRP
    chunks = kl // DCH
    d = lax.axis_index("dp")
    t = lax.axis_index("tensor")
    z = t // 2
    x = t % 2
    peer = {"dp": 1 - d}
    xnbr = {"tensor": z * 2 + (1 - x)}

    def zdev(i):
        return {"tensor": lax.rem(z + i, Z) * 2 + x}

    def zsrc(i):
        return lax.rem(z + Z - i, Z)

    def slot(j):
        return pl.ds(pl.multiple_of(j * ROWS, ROWS), ROWS)

    def remote(src, dst, ss, rs, dev):
        return pltpu.make_async_remote_copy(
            src_ref=src, dst_ref=dst, send_sem=ss, recv_sem=rs,
            device_id=dev, device_id_type=pl.DeviceIdType.MESH,
        )

    def wcopy(k):
        which, part = k // 4, k % 4
        src, dst = ((gw_hbm, gw), (uw_hbm, uw), (dw_hbm, dw))[which]
        n = src.shape[0] // 4
        return pltpu.make_async_copy(
            src.at[pl.ds(part * n, n), :], dst.at[pl.ds(part * n, n), :], w_sem.at[k]
        )

    for k in range(AHEAD):
        wcopy(k).start()

    barrier = pltpu.get_barrier_semaphore()
    for dev in [peer, xnbr] + [zdev(i) for i in range(1, Z)]:
        pl.semaphore_signal(barrier, inc=1, device_id=dev, device_id_type=pl.DeviceIdType.MESH)

    values = tok[...].astype(F32)
    average = jnp.mean(values, axis=1, keepdims=True)
    centered = values - average
    variance = jnp.mean(centered * centered, axis=1, keepdims=True)
    nrm[...] = (centered * lax.rsqrt(variance + EPSILON) * gain[...]).astype(BF16)

    pl.semaphore_wait(barrier, Z + 1)

    def cols(o):
        return pl.ds(pl.multiple_of(o * kl, kl), kl)

    first = remote(nrm.at[:, cols(1 - d)], xbuf.at[d, slot(z), :], in_s, in_r, peer)
    first.start()
    xbuf[d, slot(z), :] = nrm[:, cols(d)]
    remote(nrm.at[:, cols(d)], xbuf.at[1 - d, slot(z), :], in_s, in_r, peer).wait_recv()

    def block(h, j, u):
        return xbuf.at[h, slot(j), pl.ds(u * (kl // SUB), kl // SUB)]

    def agz(h, j, side, s, u):
        to = {"tensor": (z + 1 - 2 * side) * 2 + x}
        return remote(block(h, j, u), block(h, j, u), agz_s.at[h, side, s * SUB + u],
                      agz_r.at[h, j * SUB + u], to)

    def agx(h, j, u):
        return remote(block(h, j, u), block(h, Z + j, u), agx_s.at[h, j * SUB + u],
                      agx_r.at[h, j * SUB + u], xnbr)

    def relay(h, s, u, act):
        pl.when((z >= s) & (z < Z - 1))(lambda: act(agz(h, z - s, 0, s, u)))
        pl.when((z + s < Z) & (z > 0))(lambda: act(agz(h, z + s, 1, s, u)))

    def ag_start(h):
        for u in range(SUB):
            relay(h, 0, u, lambda c: c.start())
            agx(h, z, u).start()

    def ag_hop(h, s):
        for u in range(SUB):
            @pl.when(z >= s)
            def _():
                agz(h, z - s, 0, s, u).wait_recv()
                pl.when(z < Z - 1)(lambda: agz(h, z - s, 0, s, u).start())
                agx(h, z - s, u).start()

            @pl.when(z + s < Z)
            def _():
                agz(h, z + s, 1, s, u).wait_recv()
                pl.when(z > 0)(lambda: agz(h, z + s, 1, s, u).start())
                agx(h, z + s, u).start()

    def ag_finish(h):
        for j in range(Z):
            for u in range(SUB):
                agx(h, j, u).wait_recv()

    def prune(k):
        wcopy(k).wait()
        if k + AHEAD < 12:
            wcopy(k + AHEAD).start()
        which, part = k // 4, k % 4
        w = (gw, uw, dw)[which]
        m = (gm, um, dm)[which]
        nr, nc = w.shape[0] // BLK, w.shape[1] // BLK
        if which == 2:
            r0, c0 = t * nr, d * nc
        else:
            r0, c0 = d * nr, t * nc
        n = nr // 4

        def body(b, carry):
            rb = part * n + b
            rows = pl.ds(pl.multiple_of(rb * BLK, BLK), BLK)
            for cb in range(nc):
                keep = jnp.full((16, BLK), m[r0 + rb, c0 + cb].astype(F32), F32).astype(BF16)
                tile = w[rows, cb * BLK:(cb + 1) * BLK].reshape(BLK // 16, 16, BLK)
                w[rows, cb * BLK:(cb + 1) * BLK] = (tile * keep[None]).reshape(BLK, BLK)
            return carry

        lax.fori_loop(0, n, body, 0)

    def group(h, q, mine):
        base = (d if mine else 1 - d) * half + q * GRP

        def body(c, carry):
            cs = pl.ds(pl.multiple_of(base + c * NC, NC), NC)
            g = jnp.dot(xbuf[h], gw[:, cs], preferred_element_type=F32)
            u = jnp.dot(xbuf[h], uw[:, cs], preferred_element_type=F32)
            os = pl.ds(pl.multiple_of(c * NC, NC), NC)
            dst = own if mine else exs
            dst[q, 0, :, os] = g
            dst[q, 1, :, os] = u
            return carry

        lax.fori_loop(0, GRP // NC, body, 0)
        if not mine:
            ex(h, q).start()

    def ex(h, q):
        return remote(exs.at[q], exr.at[q], ex_s.at[h, q], ex_r.at[h, q], peer)

    def hcols(o, q):
        return pl.ds(pl.multiple_of(o * half + q * GRP, GRP), GRP)

    def hd(h, q, o):
        blk = hid.at[:, hcols(o, q)]
        return remote(blk, blk, hd_s.at[h, q], hd_r.at[h, q], peer)

    def hidden(h):
        for q in range(groups):
            ex(h, q).wait()
            g = own[q, 0] + exr[q, 0]
            u = own[q, 1] + exr[q, 1]
            hid[:, hcols(d, q)] = (g / (1.0 + jnp.exp(-g)) * u).astype(BF16)
            hd(h, q, d).start()
        for q in range(groups):
            hd(h, q, 1 - d).wait_recv()

    def chunk(c):
        return pl.ds(c * DCH, DCH)

    def rsx(h, c):
        return remote(sb.at[:, chunk(c)], rx.at[h, :, chunk(c)], rx_s.at[h, c], rx_r.at[h, c], xnbr)

    def down(h):
        for c in range(chunks):
            def body(j, carry):
                cs = pl.ds(pl.multiple_of(c * DCH + j * NC, NC), NC)
                p = jnp.dot(hid[...], dw[:, cs], preferred_element_type=F32)
                acc[:, cs] = p[:line]
                sb[:, cs] = p[line:].astype(BF16)
                return carry

            lax.fori_loop(0, DCH // NC, body, 0)
            rsx(h, c).start()
        for q in range(groups):
            hd(h, q, d).wait_send()

    def rsz(h, c, i):
        return remote(zs.at[slot(lax.rem(z + i, Z)), chunk(c)], zr.at[h, i - 1, :, chunk(c)],
                      rz_s.at[h, c, i - 1], rz_r.at[h, c, i - 1], zdev(i))

    def rs_step(h, c):
        rsx(h, c).wait()
        total = acc[:, chunk(c)] + rx[h, :, chunk(c)].astype(F32)
        acc[:, chunk(c)] = total
        zs[:, chunk(c)] = total.astype(BF16)
        for i in range(1, Z):
            rsz(h, c, i).start()

    def rs_final(h):
        for c in range(chunks):
            for i in range(1, Z):
                rsz(h, c, i).wait()
            total = acc[slot(z), chunk(c)]
            for i in range(1, Z):
                total = total + zr[h, i - 1, :, chunk(c)].astype(F32)
            fin[h, :, chunk(c)] = total.astype(BF16)

    ag_start(0)
    order = list(range(12))
    for s in range(1, Z):
        for k in order[:1]:
            prune(k)
        order = order[1:]
        ag_hop(0, s)
    ag_start(1)
    for k in order:
        prune(k)
    ag_finish(0)
    plan = [(q, False) for q in range(groups)] + [(q, True) for q in range(groups)]
    for n, (q, mine) in enumerate(plan):
        if n + 1 < Z:
            ag_hop(1, n + 1)
        group(0, q, mine)
    hidden(0)
    down(0)
    ag_finish(1)
    for n, (q, mine) in enumerate(plan):
        group(1, q, mine)
        rs_step(0, n)
    hidden(1)
    rs_final(0)
    down(1)
    for c in range(chunks):
        rs_step(1, c)
    rs_final(1)

    last = remote(fin.at[1 - d], finrx, fn_s, fn_r, peer)
    last.start()
    out[:, cols(d)] = fin[d]
    last.wait()
    out[:, cols(1 - d)] = finrx[...]
    first.wait_send()
    for h in range(2):
        for j in range(Z):
            for u in range(SUB):
                agx(h, j, u).wait_send()
                relay(h, j, u, lambda c: c.wait_send())


def fused(Z, tokens, ln_gain, gate_weight, up_weight, down_weight, gate_mask, up_mask, down_mask):
    kl, fl = gate_weight.shape
    dim = tokens.shape[1]
    half = fl // 2
    groups = half // GRP
    chunks = kl // DCH
    line = Z * ROWS
    m = 2 * line
    dma = pltpu.SemaphoreType.DMA
    vm = pl.BlockSpec(memory_space=pltpu.VMEM)
    sm = pl.BlockSpec(memory_space=pltpu.SMEM)
    hbm = pl.BlockSpec(memory_space=pl.ANY)
    flops = 2 * 2 * m * kl * fl * 3
    return pl.pallas_call(
        functools.partial(fused_kernel, Z),
        out_shape=jax.ShapeDtypeStruct((ROWS, dim), BF16),
        in_specs=[sm, sm, sm, vm, vm, hbm, hbm, hbm],
        out_specs=vm,
        scratch_shapes=[
            pltpu.VMEM((kl, fl), BF16),
            pltpu.VMEM((kl, fl), BF16),
            pltpu.VMEM((fl, kl), BF16),
            pltpu.VMEM((ROWS, dim), BF16),
            pltpu.VMEM((2, m, kl), BF16),
            pltpu.VMEM((groups, 2, m, GRP), F32),
            pltpu.VMEM((groups, 2, m, GRP), F32),
            pltpu.VMEM((groups, 2, m, GRP), F32),
            pltpu.VMEM((m, fl), BF16),
            pltpu.VMEM((line, kl), BF16),
            pltpu.VMEM((line, kl), F32),
            pltpu.VMEM((2, line, kl), BF16),
            pltpu.VMEM((line, kl), BF16),
            pltpu.VMEM((2, Z - 1, ROWS, kl), BF16),
            pltpu.VMEM((2, ROWS, kl), BF16),
            pltpu.VMEM((ROWS, kl), BF16),
            dma((12,)),
            dma, dma,
            dma((2, 2, Z * SUB)), dma((2, Z * SUB)),
            dma((2, Z * SUB)), dma((2, Z * SUB)),
            dma((2, groups)), dma((2, groups)),
            dma((2, groups)), dma((2, groups)),
            dma((2, chunks)), dma((2, chunks)),
            dma((2, chunks, Z - 1)), dma((2, chunks, Z - 1)),
            dma, dma,
        ],
        compiler_params=pltpu.CompilerParams(
            collective_id=0, has_side_effects=True, vmem_limit_bytes=63 * 1024 * 1024
        ),
        cost_estimate=pl.CostEstimate(
            flops=flops, bytes_accessed=6 * kl * fl, transcendentals=0
        ),
    )(gate_mask, up_mask, down_mask, tokens, ln_gain.reshape(1, dim),
      gate_weight, up_weight, down_weight)


def solution(mesh):
    tensor = mesh.shape["tensor"]
    owners = mesh.shape["dp"]
    copies = mesh.shape["groups"]
    Z = tensor // 2

    def per_device(tokens, ln_gain, gate_weight, *rest):
        rows = tokens.shape[0]
        kl, fl = gate_weight.shape
        fits = (
            owners == 2 and tensor == 2 * Z and rows == ROWS and Z == 4
            and kl == 4 * DCH and fl == 4 * GRP
        )
        if fits:
            return fused(Z, tokens, ln_gain, gate_weight, *rest)
        return general(tokens, ln_gain, gate_weight, *rest)

    in_specs = (
        P(("groups", "dp", "tensor"), None),
        P(),
        P("dp", "tensor"),
        P("dp", "tensor"),
        P("tensor", "dp"),
        P(),
        P(),
        P(),
    )
    out_specs = P(("groups", "dp", "tensor"), None)
    return jax.shard_map(
        per_device, mesh=mesh, in_specs=in_specs, out_specs=out_specs, check_vma=False
    )
```
